256 devices in a mesh: ctx: 32 (over z, x), tp: 8 (over y, core).
Axes of the slice: x: 4, y: 4, z: 8, core: 2. Of those that a mesh axis runs over, the one named last changes fastest.
Arguments:
- attn_query: bfloat16 [8192, 4096], P('ctx', 'tp'), may hold values from -8 to 8
- attn_key: bfloat16 [8192, 4096], P('ctx', 'tp'), may hold values from -8 to 8
- attn_value: bfloat16 [8192, 4096], P('ctx', 'tp'), may hold values from -6 to 6
- out_weight: bfloat16 [4096, 8192], P('tp'), may hold values from -0.125 to 0.125
Outputs:
- attn_out: bfloat16 [8192, 8192], P('ctx', 'tp')
The draws below stay inside these ranges and needn't reach their ends.
All inputs are finite; a program needn't handle non-finite values.
Results may differ from the reference program's by a relative error of at most 0.015.
Values may be sent and summed in bfloat16 or wider, within the bound.
A program may use at most 128 MiB of HBM per device.

```python
import jax
import jax.numpy as jnp
from jax import lax

D = 8192
HEADS = 32
HD = 128
SEQ = 8192
N_TP = 8


def draw_attn_query(key, part):
    width = HEADS * HD
    base = jnp.clip(jax.random.normal(jax.random.fold_in(key, 1), (SEQ, width), jnp.float32), -8.0, 8.0)
    return base.astype(jnp.bfloat16)


def draw_attn_key(key, part):
    width = HEADS * HD
    base = jnp.clip(jax.random.normal(jax.random.fold_in(key, 2), (SEQ, width), jnp.float32), -8.0, 8.0)
    return base.astype(jnp.bfloat16)


def strengthened(values, key, source, target, blocks, factor):
    owner, partner = [(jnp.arange(values.shape[axis_at]) // (values.shape[axis_at] // blocks)).reshape([-1 if axis == axis_at else 1 for axis in range(values.ndim)]) for axis_at in (source, target)]
    chosen = jax.random.permutation(key, blocks)[partner]
    strong = (owner == chosen) | (owner == (partner + blocks // 2) % blocks)
    return jnp.where(strong, factor * values, values)


def block_levels(own_key, dims, pieces, low, top_value):
    level, own = 1.0, jax.random.fold_in(own_key, 6)
    for axis_at, blocks in pieces:
        steps = jnp.exp(jax.random.uniform(jax.random.fold_in(own, axis_at), (blocks,), jnp.float32, low / len(pieces), top_value / len(pieces)))
        level = level * jnp.repeat(steps, dims[axis_at] // blocks).reshape([-1 if axis == axis_at else 1 for axis in range(len(dims))])
    return level


def centred(stream_key, shape, scale, most, shards=(), held_as=jnp.bfloat16):
    array = scale * jax.random.normal(stream_key, shape, jnp.float32)
    if shards:
        array = array * block_levels(stream_key, shape, shards, -0.22, 0.18)
    return jnp.clip(array, -most, most).astype(held_as)


def bell_draw_with(own_key, extent, scale, bound, cuts, heavy, kind=jnp.bfloat16):
    array = scale * jax.random.normal(own_key, extent, jnp.float32)
    if cuts:
        array = array * block_levels(own_key, extent, cuts, -0.22, 0.18)
    return jnp.clip(strengthened(array, jax.random.fold_in(own_key, 3), *heavy), -bound, bound).astype(kind)


def setup_inputs(seed: int = 0) -> dict:
    arg_keys = jax.random.split(jax.random.key(seed), 5)
    return {
        "attn_query": draw_attn_query(jax.random.fold_in(arg_keys[4], 71), 0),
        "attn_key": draw_attn_key(jax.random.fold_in(arg_keys[4], 71), 0),
        "attn_value": centred(arg_keys[2], (SEQ, HEADS * HD), 1.0, 6.0, ((0, 32), (1, 8))),
        "out_weight": bell_draw_with(arg_keys[3], (HEADS * HD, D), (HEADS * HD) ** -0.5, 0.125, ((0, 8),), (0, 1, 8, 2.0)),
    }


def reference(attn_query, attn_key, attn_value, out_weight):
    scale = HD ** -0.5
    span_rows = 512 if SEQ % 512 == 0 else SEQ
    queries = attn_query.reshape(SEQ, HEADS, HD).astype(jnp.float32)
    keys = attn_key.reshape(SEQ, HEADS, HD).astype(jnp.float32)
    values = attn_value.reshape(SEQ, HEADS, HD).astype(jnp.float32)
    key_pos = jnp.arange(SEQ, dtype=jnp.int32)

    def one_block(start):
        block = lax.dynamic_slice_in_dim(queries, start, span_rows, 0)
        query_pos = start + jnp.arange(span_rows, dtype=jnp.int32)
        scores = jnp.einsum("qhd,khd->hqk", block, keys) * scale
        allowed = key_pos[None, None, :] <= query_pos[None, :, None]
        largest = jnp.max(jnp.where(allowed, scores, -1e30), axis=-1)
        weights = jnp.where(allowed, jnp.exp(scores - largest[..., None]), 0.0)
        totals = jnp.sum(weights, axis=-1)
        probs = weights.astype(jnp.bfloat16).astype(jnp.float32)
        numer = jnp.einsum("hqk,khd->qhd", probs, values)
        return (numer / jnp.transpose(totals)[..., None]).astype(jnp.bfloat16)

    starts = jnp.arange(SEQ // span_rows, dtype=jnp.int32) * span_rows
    heads = lax.map(one_block, starts).reshape(SEQ, HEADS * HD)

    group = HEADS * HD // N_TP

    def add_group(index, total):
        cols = lax.dynamic_slice_in_dim(heads, index * group, group, 1)
        rows = lax.dynamic_slice_in_dim(out_weight, index * group, group, 0)
        partial_value = jnp.dot(cols, rows, preferred_element_type=jnp.float32).astype(jnp.bfloat16)
        partial_value = lax.optimization_barrier(partial_value)
        return total + partial_value.astype(jnp.float32)

    summed = lax.fori_loop(0, N_TP, add_group, jnp.zeros((SEQ, D), jnp.float32))
    return summed.astype(jnp.bfloat16)
```

```python
import functools

import jax
import jax.numpy as jnp
from jax import lax
from jax.experimental import pallas as pl
from jax.experimental.pallas import tpu as pltpu
from jax.sharding import PartitionSpec as P

HD = 128
NX, NY, NZ, NC = 4, 4, 8, 2
ROWS = 256
HALF = ROWS // NC
COLS = 1024
CHUNK = 256
NCH = COLS // CHUNK
KEYS = NX * ROWS
LOG2E = 1.4426950408889634
C2 = (HD ** -0.5) * LOG2E
F32 = jnp.float32
BF16 = jnp.bfloat16


def wait_for(ref, sem):
    pltpu.make_async_copy(ref, ref, sem).wait()


def kernel(
    q_hbm, k_hbm, v_hbm, w_hbm, out_ref,
    src, qb, kv, wb, heads, obuf, acc, mx, sm, pbuf, ropp, rfin,
    s_load, s_w, r_w, ss_w,
    s_q, s_kv, r_q, r_kv,
    s_x, r_x, s_rel, r_rel,
    s_o, r_o, s_oc, r_oc,
    s_p, r_p,
):
    ctx = lax.axis_index("ctx")
    tp = lax.axis_index("tp")
    z, x = ctx // NX, ctx % NX
    y, c = tp // NC, tp % NC
    xr, xl, xo = (x + 1) % NX, (x + 3) % NX, (x + 2) % NX
    yr, yl, yo = (y + 1) % NY, (y + 3) % NY, (y + 2) % NY
    sib = 1 - c

    def dev(x_, y_, z_, c_):
        return {"ctx": z_ * NX + x_, "tp": y_ * NC + c_}

    def remote(src_ref, dst_ref, send, recv, where):
        return pltpu.make_async_remote_copy(
            src_ref=src_ref, dst_ref=dst_ref, send_sem=send, recv_sem=recv,
            device_id=where, device_id_type=pl.DeviceIdType.MESH,
        )

    right, left, across = dev(xr, y, z, c), dev(xl, y, z, c), dev(x, y, z, sib)
    up, down = dev(x, yr, z, c), dev(x, yl, z, c)

    for n, hbm in enumerate((q_hbm, k_hbm, v_hbm)):
        for j in range(4):
            for h in range(NC):
                pltpu.make_async_copy(
                    hbm.at[pl.ds(h * HALF, HALF), pl.ds(j * HD, HD)], src.at[j, h, n], s_load.at[j, h, n]
                ).start()

    barrier = pltpu.get_barrier_semaphore()
    for k in range(1, NZ * NC):
        other = (z * NC + c + k) % (NZ * NC)
        pl.semaphore_signal(barrier, inc=1, device_id=dev(x, y, other // NC, other % NC), device_id_type=pl.DeviceIdType.MESH)
    for other in (right, left, up, down):
        pl.semaphore_signal(barrier, inc=1, device_id=other, device_id_type=pl.DeviceIdType.MESH)

    acc[...] = jnp.zeros(acc.shape, F32)
    sm[...] = jnp.zeros(sm.shape, F32)
    mx[...] = jnp.full(mx.shape, -1e30, F32)
    for j in range(4):
        for h in range(NC):
            for n in range(3):
                wait_for(src.at[j, h, n], s_load.at[j, h, n])
    pl.semaphore_wait(barrier, NZ * NC - 1 + 4)

    def zof(s):
        return (z + ((s + 1) // 2) * (1 - 2 * ((s + 1) % 2)) + NZ) % NZ

    def send_heads(s, carry):
        zd = zof(s)

        @pl.when(zd // 4 == c)
        def _():
            j = zd - 4 * c
            for k in range(NC):
                cd = (c + 1 - k) % NC

                def go():
                    remote(src.at[j, cd, 0], qb.at[z], s_q.at[j, k], r_q.at[z], dev(x, y, zd, cd)).start()
                    remote(src.at[j, cd, pl.ds(1, 2)], kv.at[z, x * NC + cd], s_kv.at[j, k], r_kv.at[z], dev(x, y, zd, cd)).start()

                if k == 0:
                    go()
                else:
                    pl.when(zd != z)(go)

                    @pl.when(zd == z)
                    def _():
                        pltpu.make_async_copy(src.at[j, cd, 0], qb.at[z], r_q.at[z]).start()
                        pltpu.make_async_copy(src.at[j, cd, pl.ds(1, 2)], kv.at[z, x * NC + cd], r_kv.at[z]).start()

        return carry

    lax.fori_loop(0, NZ, send_heads, 0)

    for n in range(NY):
        pltpu.make_async_copy(
            w_hbm.at[:, pl.ds((n * NC + c) * COLS, COLS)], wb.at[n, c], s_w.at[n]
        ).start()

    def unit(zq, zk, diagonal):
        query = qb[zq]
        key = kv[zk, :, 0].reshape(KEYS, HD)
        value = kv[zk, :, 1].reshape(KEYS, HD)
        scores = lax.dot_general(query, key, (((1,), (1,)), ((), ())), preferred_element_type=F32)
        if diagonal:
            row = lax.broadcasted_iota(jnp.int32, scores.shape, 0)
            col = lax.broadcasted_iota(jnp.int32, scores.shape, 1)
            scores = jnp.where(col <= row + (x * NC + c) * HALF, scores, -1e30)
        old = mx[zq]
        new = jnp.maximum(old, jnp.max(scores, axis=1, keepdims=True))
        factor = jnp.exp2((old - new) * C2)
        weights = jnp.exp2((scores - jnp.concatenate([new] * (KEYS // HD), axis=1)) * C2)
        mx[zq] = new
        sm[zq] = sm[zq] * factor + jnp.sum(weights, axis=1, keepdims=True)
        acc[zq] = acc[zq] * factor + jnp.dot(weights.astype(BF16), value, preferred_element_type=F32)

    def step(s, carry):
        @pl.when(s < NZ)
        def _():
            zs = zof(s)
            mine = kv.at[zs, x * NC + c]
            wait_for(qb.at[zs], r_q.at[zs])
            wait_for(mine, r_kv.at[zs])
            remote(mine, mine, s_x.at[zs, 0], r_x.at[zs, 0], right).start()
            remote(mine, mine, s_x.at[zs, 1], r_x.at[zs, 1], left).start()
            remote(mine, mine, s_rel.at[zs, 0], r_rel.at[zs, 0], across).start()

        @pl.when((s >= 1) & (s < NZ + 1))
        def _():
            zs = zof(s - 1)
            a = kv.at[zs, xl * NC + c]
            wait_for(a, r_x.at[zs, 0])
            remote(a.at[0], a.at[0], s_x.at[zs, 2], r_x.at[zs, 2], right).start()
            remote(a, a, s_rel.at[zs, 1], r_rel.at[zs, 1], across).start()
            b = kv.at[zs, xr * NC + c]
            wait_for(b, r_x.at[zs, 1])
            remote(b.at[1], b.at[1], s_x.at[zs, 3], r_x.at[zs, 3], left).start()
            remote(b, b, s_rel.at[zs, 2], r_rel.at[zs, 2], across).start()

        @pl.when((s >= 2) & (s < NZ + 2))
        def _():
            zs = zof(s - 2)
            o = kv.at[zs, xo * NC + c]
            wait_for(o.at[0], r_x.at[zs, 2])
            wait_for(o.at[1], r_x.at[zs, 3])
            remote(o, o, s_rel.at[zs, 3], r_rel.at[zs, 3], across).start()

        @pl.when((s >= 2) & (s < 2 + NY))
        def _():
            n = s - 2
            remote(
                w_hbm.at[:, pl.ds((n * NC + sib) * COLS, COLS)], wb.at[n, c], ss_w.at[n], r_w.at[n], across
            ).start()

        @pl.when(s >= 3)
        def _():
            t = s - 3
            zs = zof(t)
            for n, xx in enumerate((x, xl, xr, xo)):
                wait_for(kv.at[zs, xx * NC + sib], r_rel.at[zs, n])
            unit(zs, zs, True)

            def earlier(u, inner):
                zu = zof(u)
                unit(jnp.maximum(zs, zu), jnp.minimum(zs, zu), False)
                return inner

            lax.fori_loop(0, t, earlier, 0)

        return carry

    lax.fori_loop(0, NZ + 3, step, 0)

    def send_out(s, carry):
        zs = zof(NZ - 1 - s)
        obuf[zs] = (acc[zs] / sm[zs]).astype(BF16)
        spot = heads.at[pl.ds(c * HALF, HALF), pl.ds(z * HD, HD)]

        @pl.when(zs != z)
        def _():
            remote(obuf.at[zs], spot, s_o.at[zs], r_o.at[z], dev(x, y, zs, c)).start()

        @pl.when(zs == z)
        def _():
            pltpu.make_async_copy(obuf.at[zs], spot, r_o.at[z]).start()

        return carry

    lax.fori_loop(0, NZ, send_out, 0)

    def relay_out(s, carry):
        h = zof(s)
        spot = heads.at[pl.ds(c * HALF, HALF), pl.ds(h * HD, HD)]
        wait_for(spot, r_o.at[h])
        remote(spot, spot, s_oc.at[h], r_oc.at[h], across).start()
        return carry

    lax.fori_loop(0, NZ, relay_out, 0)
    for n in range(NY):
        wait_for(wb.at[n, c], s_w.at[n])
        wait_for(wb.at[n, sib], r_w.at[n])

    def await_out(s, carry):
        h = zof(s)
        wait_for(heads.at[pl.ds(sib * HALF, HALF), pl.ds(h * HD, HD)], r_oc.at[h])
        return carry

    lax.fori_loop(0, NZ, await_out, 0)

    def project(n, k):
        cols = slice(k * CHUNK, (k + 1) * CHUNK)
        weight = jnp.concatenate([wb[n, 0, :, cols], wb[n, 1, :, cols]], axis=0)
        return jnp.dot(heads[...], weight, preferred_element_type=F32)

    for k in range(NCH):
        pbuf[0, k] = project(yo, k).astype(BF16)
        remote(pbuf.at[0, k], ropp.at[k], s_p.at[0, k], r_p.at[0, k], up if k < NCH // 2 else down).start()
    half = NCH // 2
    for k in range(half):
        a, b = half + k, k
        pbuf[1, a] = project(yr, a).astype(BF16)
        remote(pbuf.at[1, a], rfin.at[0, a], s_p.at[1, a], r_p.at[1, a], up).start()
        pbuf[2, b] = project(yl, b).astype(BF16)
        remote(pbuf.at[2, b], rfin.at[1, b], s_p.at[2, b], r_p.at[2, b], down).start()
    for k in range(half):
        a, b = k, half + k
        part = project(yr, a)
        wait_for(ropp.at[a], r_p.at[0, a])
        pbuf[1, a] = (part + ropp[a].astype(F32)).astype(BF16)
        remote(pbuf.at[1, a], rfin.at[0, a], s_p.at[1, a], r_p.at[1, a], up).start()
        part = project(yl, b)
        wait_for(ropp.at[b], r_p.at[0, b])
        pbuf[2, b] = (part + ropp[b].astype(F32)).astype(BF16)
        remote(pbuf.at[2, b], rfin.at[1, b], s_p.at[2, b], r_p.at[2, b], down).start()
    order = [2, 0, 3, 1]
    for k in order:
        part = project(y, k)
        wait_for(rfin.at[0, k], r_p.at[1, k])
        wait_for(rfin.at[1, k], r_p.at[2, k])
        out_ref[:, k * CHUNK : (k + 1) * CHUNK] = (
            part + rfin[0, k].astype(F32) + rfin[1, k].astype(F32)
        ).astype(BF16)

    def drain(s, carry):
        zs = zof(s)

        @pl.when(zs // 4 == c)
        def _():
            j = zs - 4 * c
            wait_for(src.at[j, sib, 0], s_q.at[j, 0])
            wait_for(src.at[j, sib, pl.ds(1, 2)], s_kv.at[j, 0])

            @pl.when(zs != z)
            def _():
                wait_for(src.at[j, c, 0], s_q.at[j, 1])
                wait_for(src.at[j, c, pl.ds(1, 2)], s_kv.at[j, 1])

        for n, xx in enumerate((x, x, xl, xr)):
            part = kv.at[zs, xx * NC + c]
            wait_for(part if n < 2 else part.at[n - 2], s_x.at[zs, n])
        for n, xx in enumerate((x, xl, xr, xo)):
            wait_for(kv.at[zs, xx * NC + c], s_rel.at[zs, n])

        @pl.when(zs != z)
        def _():
            wait_for(obuf.at[zs], s_o.at[zs])

        wait_for(heads.at[pl.ds(c * HALF, HALF), pl.ds(zs * HD, HD)], s_oc.at[zs])
        return carry

    lax.fori_loop(0, NZ, drain, 0)
    for n in range(NY):
        wait_for(w_hbm.at[:, pl.ds((n * NC + sib) * COLS, COLS)], ss_w.at[n])
    for k in range(NCH):
        for n in range(3):
            wait_for(pbuf.at[n, k], s_p.at[n, k])


def per_device(attn_query, attn_key, attn_value, out_weight):
    dma = pltpu.SemaphoreType.DMA
    anywhere = pl.BlockSpec(memory_space=pl.ANY)
    return pl.pallas_call(
        kernel,
        out_shape=jax.ShapeDtypeStruct((ROWS, COLS), BF16),
        in_specs=[anywhere] * 4,
        out_specs=pl.BlockSpec(memory_space=pltpu.VMEM),
        scratch_shapes=[
            pltpu.VMEM((4, NC, 3, HALF, HD), BF16),
            pltpu.VMEM((NZ, HALF, HD), BF16),
            pltpu.VMEM((NZ, NX * NC, 2, HALF, HD), BF16),
            pltpu.VMEM((NY, NC, 512, COLS), BF16),
            pltpu.VMEM((ROWS, NZ * HD), BF16),
            pltpu.VMEM((NZ, HALF, HD), BF16),
            pltpu.VMEM((NZ, HALF, HD), F32),
            pltpu.VMEM((NZ, HALF, HD), F32),
            pltpu.VMEM((NZ, HALF, HD), F32),
            pltpu.VMEM((3, NCH, ROWS, CHUNK), BF16),
            pltpu.VMEM((NCH, ROWS, CHUNK), BF16),
            pltpu.VMEM((2, NCH, ROWS, CHUNK), BF16),
            dma((4, NC, 3)), dma((NY,)), dma((NY,)), dma((NY,)),
            dma((4, NC)), dma((4, NC)), dma((NZ,)), dma((NZ,)),
            dma((NZ, 4)), dma((NZ, 4)), dma((NZ, 4)), dma((NZ, 4)),
            dma((NZ,)), dma((NZ,)), dma((NZ,)), dma((NZ,)),
            dma((3, NCH)), dma((3, NCH)),
        ],
        compiler_params=pltpu.CompilerParams(
            collective_id=0, has_side_effects=True, vmem_limit_bytes=56 << 20
        ),
        name="attention",
    )(attn_query, attn_key, attn_value, out_weight)


def solution(mesh):
    return jax.shard_map(
        per_device,
        mesh=mesh,
        in_specs=(P("ctx", "tp"), P("ctx", "tp"), P("ctx", "tp"), P("tp", None)),
        out_specs=P("ctx", "tp"),
        check_vma=False,
    )
```

```python
import functools

import jax
import jax.numpy as jnp
from jax import lax
from jax.experimental import pallas as pl
from jax.experimental.pallas import tpu as pltpu
from jax.sharding import PartitionSpec as P

HD = 128
NX, NY, NZ, NC = 4, 4, 8, 2
ROWS = 256
HALF = ROWS // NC
COLS = 1024
CHUNK = 256
NCH = COLS // CHUNK
KEYS = NX * ROWS
LOG2E = 1.4426950408889634
C2 = (HD ** -0.5) * LOG2E
F32 = jnp.float32
BF16 = jnp.bfloat16


def wait_for(ref, sem):
    pltpu.make_async_copy(ref, ref, sem).wait()


def kernel(
    q_hbm, k_hbm, v_hbm, w_hbm, out_ref,
    src, qkv, wb, heads, obuf, acc, mx, sm, pbuf, ropp, rfin,
    s_load, s_w, r_w, ss_w,
    s_z, r_z,
    s_x, r_x, s_rel, r_rel,
    s_o, r_o, s_oc, r_oc,
    s_p, r_p,
):
    ctx = lax.axis_index("ctx")
    tp = lax.axis_index("tp")
    z, x = ctx // NX, ctx % NX
    y, c = tp // NC, tp % NC
    xr, xl, xo = (x + 1) % NX, (x + 3) % NX, (x + 2) % NX
    yr, yl, yo = (y + 1) % NY, (y + 3) % NY, (y + 2) % NY
    sib = 1 - c

    def dev(x_, y_, z_, c_):
        return {"ctx": z_ * NX + x_, "tp": y_ * NC + c_}

    def remote(src_ref, dst_ref, send, recv, where):
        return pltpu.make_async_remote_copy(
            src_ref=src_ref, dst_ref=dst_ref, send_sem=send, recv_sem=recv,
            device_id=where, device_id_type=pl.DeviceIdType.MESH,
        )

    right, left, across = dev(xr, y, z, c), dev(xl, y, z, c), dev(x, y, z, sib)
    up, down = dev(x, yr, z, c), dev(x, yl, z, c)

    for n, hbm in enumerate((q_hbm, k_hbm, v_hbm)):
        for j in range(4):
            for h in range(NC):
                pltpu.make_async_copy(
                    hbm.at[pl.ds(h * HALF, HALF), pl.ds(j * HD, HD)], src.at[j, h, n], s_load.at[j, h, n]
                ).start()

    barrier = pltpu.get_barrier_semaphore()
    for k in range(1, NZ * NC):
        other = (z * NC + c + k) % (NZ * NC)
        pl.semaphore_signal(barrier, inc=1, device_id=dev(x, y, other // NC, other % NC), device_id_type=pl.DeviceIdType.MESH)
    for other in (right, left, up, down):
        pl.semaphore_signal(barrier, inc=1, device_id=other, device_id_type=pl.DeviceIdType.MESH)

    acc[...] = jnp.zeros(acc.shape, F32)
    sm[...] = jnp.zeros(sm.shape, F32)
    mx[...] = jnp.full(mx.shape, -1e30, F32)
    for j in range(4):
        for h in range(NC):
            for n in range(3):
                wait_for(src.at[j, h, n], s_load.at[j, h, n])
    pl.semaphore_wait(barrier, NZ * NC - 1 + 4)

    def zof(s):
        return (z + ((s + 1) // 2) * (1 - 2 * ((s + 1) % 2)) + NZ) % NZ

    def send_heads(s, carry):
        zd = zof(s)

        @pl.when(zd // 4 == c)
        def _():
            j = zd - 4 * c
            for k in range(NC):
                cd = (c + 1 - k) % NC

                def go():
                    remote(src.at[j, cd], qkv.at[z, x * NC + cd], s_z.at[j, k], r_z.at[z], dev(x, y, zd, cd)).start()

                if k == 0:
                    go()
                else:
                    pl.when(zd != z)(go)

                    @pl.when(zd == z)
                    def _():
                        pltpu.make_async_copy(src.at[j, cd], qkv.at[z, x * NC + cd], r_z.at[z]).start()

        return carry

    lax.fori_loop(0, NZ, send_heads, 0)

    for n in range(NY):
        pltpu.make_async_copy(
            w_hbm.at[:, pl.ds((n * NC + c) * COLS, COLS)], wb.at[n, c], s_w.at[n]
        ).start()

    def pair(zs, xx, core):
        return qkv.at[zs, xx * NC + core, pl.ds(1, 2)]

    def one(zs, xx, n):
        return qkv.at[zs, xx * NC + c, 1 + n]

    def unit(zq, zk, diagonal):
        query = qkv[zq, x * NC + c, 0]
        key = qkv[zk, :, 1].reshape(KEYS, HD)
        value = qkv[zk, :, 2].reshape(KEYS, HD)
        scores = lax.dot_general(query, key, (((1,), (1,)), ((), ())), preferred_element_type=F32)
        if diagonal:
            row = lax.broadcasted_iota(jnp.int32, scores.shape, 0)
            col = lax.broadcasted_iota(jnp.int32, scores.shape, 1)
            scores = jnp.where(col <= row + (x * NC + c) * HALF, scores, -1e30)
        old = mx[zq]
        new = jnp.maximum(old, jnp.max(scores, axis=1, keepdims=True))
        factor = jnp.exp2((old - new) * C2)
        weights = jnp.exp2((scores - jnp.concatenate([new] * (KEYS // HD), axis=1)) * C2)
        mx[zq] = new
        sm[zq] = sm[zq] * factor + jnp.sum(weights, axis=1, keepdims=True)
        acc[zq] = acc[zq] * factor + jnp.dot(weights.astype(BF16), value, preferred_element_type=F32)

    def step(s, carry):
        @pl.when(s < NZ)
        def _():
            zs = zof(s)
            mine = pair(zs, x, c)
            wait_for(qkv.at[zs, x * NC + c], r_z.at[zs])
            remote(mine, mine, s_x.at[zs, 0], r_x.at[zs, 0], right).start()
            remote(mine, mine, s_x.at[zs, 1], r_x.at[zs, 1], left).start()
            remote(mine, mine, s_rel.at[zs, 0], r_rel.at[zs, 0], across).start()

        @pl.when((s >= 1) & (s < NZ + 1))
        def _():
            zs = zof(s - 1)
            a = pair(zs, xl, c)
            wait_for(a, r_x.at[zs, 0])
            remote(one(zs, xl, 0), one(zs, xl, 0), s_x.at[zs, 2], r_x.at[zs, 2], right).start()
            remote(a, a, s_rel.at[zs, 1], r_rel.at[zs, 1], across).start()
            b = pair(zs, xr, c)
            wait_for(b, r_x.at[zs, 1])
            remote(one(zs, xr, 1), one(zs, xr, 1), s_x.at[zs, 3], r_x.at[zs, 3], left).start()
            remote(b, b, s_rel.at[zs, 2], r_rel.at[zs, 2], across).start()

        @pl.when((s >= 2) & (s < NZ + 2))
        def _():
            zs = zof(s - 2)
            o = pair(zs, xo, c)
            wait_for(one(zs, xo, 0), r_x.at[zs, 2])
            wait_for(one(zs, xo, 1), r_x.at[zs, 3])
            remote(o, o, s_rel.at[zs, 3], r_rel.at[zs, 3], across).start()

        @pl.when(s >= NZ + 3 - NY)
        def _():
            n = s - (NZ + 3 - NY)
            remote(
                w_hbm.at[:, pl.ds((n * NC + sib) * COLS, COLS)], wb.at[n, c], ss_w.at[n], r_w.at[n], across
            ).start()

        @pl.when(s >= 3)
        def _():
            t = s - 3
            zs = zof(t)
            for n, xx in enumerate((x, xl, xr, xo)):
                wait_for(pair(zs, xx, sib), r_rel.at[zs, n])
            unit(zs, zs, True)

            def earlier(u, inner):
                zu = zof(u)
                unit(jnp.maximum(zs, zu), jnp.minimum(zs, zu), False)
                return inner

            lax.fori_loop(0, t, earlier, 0)

        return carry

    lax.fori_loop(0, NZ + 3, step, 0)

    def send_out(s, carry):
        zs = zof(NZ - 1 - s)
        obuf[zs] = (acc[zs] / sm[zs]).astype(BF16)
        spot = heads.at[pl.ds(c * HALF, HALF), pl.ds(z * HD, HD)]

        @pl.when(zs != z)
        def _():
            remote(obuf.at[zs], spot, s_o.at[zs], r_o.at[z], dev(x, y, zs, c)).start()

        @pl.when(zs == z)
        def _():
            pltpu.make_async_copy(obuf.at[zs], spot, r_o.at[z]).start()

        return carry

    lax.fori_loop(0, NZ, send_out, 0)

    def relay_out(s, carry):
        h = zof(s)
        spot = heads.at[pl.ds(c * HALF, HALF), pl.ds(h * HD, HD)]
        wait_for(spot, r_o.at[h])
        remote(spot, spot, s_oc.at[h], r_oc.at[h], across).start()
        return carry

    lax.fori_loop(0, NZ, relay_out, 0)
    for n in range(NY):
        wait_for(wb.at[n, c], s_w.at[n])
        wait_for(wb.at[n, sib], r_w.at[n])

    def await_out(s, carry):
        h = zof(s)
        wait_for(heads.at[pl.ds(sib * HALF, HALF), pl.ds(h * HD, HD)], r_oc.at[h])
        return carry

    lax.fori_loop(0, NZ, await_out, 0)

    def project(n, k):
        cols = slice(k * CHUNK, (k + 1) * CHUNK)
        weight = jnp.concatenate([wb[n, 0, :, cols], wb[n, 1, :, cols]], axis=0)
        return jnp.dot(heads[...], weight, preferred_element_type=F32)

    for k in range(NCH):
        pbuf[0, k] = project(yo, k).astype(BF16)
        remote(pbuf.at[0, k], ropp.at[k], s_p.at[0, k], r_p.at[0, k], up if k < NCH // 2 else down).start()
    half = NCH // 2
    for k in range(half):
        a, b = half + k, k
        pbuf[1, a] = project(yr, a).astype(BF16)
        remote(pbuf.at[1, a], rfin.at[0, a], s_p.at[1, a], r_p.at[1, a], up).start()
        pbuf[2, b] = project(yl, b).astype(BF16)
        remote(pbuf.at[2, b], rfin.at[1, b], s_p.at[2, b], r_p.at[2, b], down).start()
    for k in range(half):
        a, b = k, half + k
        part = project(yr, a)
        wait_for(ropp.at[a], r_p.at[0, a])
        pbuf[1, a] = (part + ropp[a].astype(F32)).astype(BF16)
        remote(pbuf.at[1, a], rfin.at[0, a], s_p.at[1, a], r_p.at[1, a], up).start()
        part = project(yl, b)
        wait_for(ropp.at[b], r_p.at[0, b])
        pbuf[2, b] = (part + ropp[b].astype(F32)).astype(BF16)
        remote(pbuf.at[2, b], rfin.at[1, b], s_p.at[2, b], r_p.at[2, b], down).start()
    order = [2, 0, 3, 1]
    for k in order:
        part = project(y, k)
        wait_for(rfin.at[0, k], r_p.at[1, k])
        wait_for(rfin.at[1, k], r_p.at[2, k])
        out_ref[:, k * CHUNK : (k + 1) * CHUNK] = (
            part + rfin[0, k].astype(F32) + rfin[1, k].astype(F32)
        ).astype(BF16)

    def drain(s, carry):
        zs = zof(s)

        @pl.when(zs // 4 == c)
        def _():
            j = zs - 4 * c
            wait_for(src.at[j, sib], s_z.at[j, 0])

            @pl.when(zs != z)
            def _():
                wait_for(src.at[j, c], s_z.at[j, 1])

        for n, xx in enumerate((x, x, xl, xr)):
            wait_for(pair(zs, xx, c) if n < 2 else one(zs, xx, n - 2), s_x.at[zs, n])
        for n, xx in enumerate((x, xl, xr, xo)):
            wait_for(pair(zs, xx, c), s_rel.at[zs, n])

        @pl.when(zs != z)
        def _():
            wait_for(obuf.at[zs], s_o.at[zs])

        wait_for(heads.at[pl.ds(c * HALF, HALF), pl.ds(zs * HD, HD)], s_oc.at[zs])
        return carry

    lax.fori_loop(0, NZ, drain, 0)
    for n in range(NY):
        wait_for(w_hbm.at[:, pl.ds((n * NC + sib) * COLS, COLS)], ss_w.at[n])
    for k in range(NCH):
        for n in range(3):
            wait_for(pbuf.at[n, k], s_p.at[n, k])


def per_device(attn_query, attn_key, attn_value, out_weight):
    dma = pltpu.SemaphoreType.DMA
    anywhere = pl.BlockSpec(memory_space=pl.ANY)
    return pl.pallas_call(
        kernel,
        out_shape=jax.ShapeDtypeStruct((ROWS, COLS), BF16),
        in_specs=[anywhere] * 4,
        out_specs=pl.BlockSpec(memory_space=pltpu.VMEM),
        scratch_shapes=[
            pltpu.VMEM((4, NC, 3, HALF, HD), BF16),
            pltpu.VMEM((NZ, NX * NC, 3, HALF, HD), BF16),
            pltpu.VMEM((NY, NC, 512, COLS), BF16),
            pltpu.VMEM((ROWS, NZ * HD), BF16),
            pltpu.VMEM((NZ, HALF, HD), BF16),
            pltpu.VMEM((NZ, HALF, HD), F32),
            pltpu.VMEM((NZ, HALF, HD), F32),
            pltpu.VMEM((NZ, HALF, HD), F32),
            pltpu.VMEM((3, NCH, ROWS, CHUNK), BF16),
            pltpu.VMEM((NCH, ROWS, CHUNK), BF16),
            pltpu.VMEM((2, NCH, ROWS, CHUNK), BF16),
            dma((4, NC, 3)), dma((NY,)), dma((NY,)), dma((NY,)),
            dma((4, NC)), dma((NZ,)),
            dma((NZ, 4)), dma((NZ, 4)), dma((NZ, 4)), dma((NZ, 4)),
            dma((NZ,)), dma((NZ,)), dma((NZ,)), dma((NZ,)),
            dma((3, NCH)), dma((3, NCH)),
        ],
        compiler_params=pltpu.CompilerParams(
            collective_id=0, has_side_effects=True, vmem_limit_bytes=56 << 20
        ),
        name="attention",
    )(attn_query, attn_key, attn_value, out_weight)


def solution(mesh):
    return jax.shard_map(
        per_device,
        mesh=mesh,
        in_specs=(P("ctx", "tp"), P("ctx", "tp"), P("ctx", "tp"), P("tp", None)),
        out_specs=P("ctx", "tp"),
        check_vma=False,
    )
```

```python
import functools

import jax
import jax.numpy as jnp
from jax import lax
from jax.experimental import pallas as pl
from jax.experimental.pallas import tpu as pltpu
from jax.sharding import PartitionSpec as P

HD = 128
NX, NY, NZ, NC = 4, 4, 8, 2
ROWS = 256
HALF = ROWS // NC
COLS = 1024
CHUNK = 256
NCH = COLS // CHUNK
KEYS = NX * ROWS
LOG2E = 1.4426950408889634
C2 = (HD ** -0.5) * LOG2E
F32 = jnp.float32
BF16 = jnp.bfloat16


def wait_for(ref, sem):
    pltpu.make_async_copy(ref, ref, sem).wait()


def kernel(
    q_hbm, k_hbm, v_hbm, w_hbm, out_ref,
    src, qkv, wb, heads, obuf, acc, mx, sm, pbuf, ropp, rfin,
    s_load, s_w, r_w, ss_w,
    s_z, r_z,
    s_x, r_x, s_rel, r_rel,
    s_o, r_o, s_oc, r_oc,
    s_p, r_p,
):
    ctx = lax.axis_index("ctx")
    tp = lax.axis_index("tp")
    z, x = ctx // NX, ctx % NX
    y, c = tp // NC, tp % NC
    xr, xl, xo = (x + 1) % NX, (x + 3) % NX, (x + 2) % NX
    yr, yl, yo = (y + 1) % NY, (y + 3) % NY, (y + 2) % NY
    sib = 1 - c

    def dev(x_, y_, z_, c_):
        return {"ctx": z_ * NX + x_, "tp": y_ * NC + c_}

    def remote(src_ref, dst_ref, send, recv, where):
        return pltpu.make_async_remote_copy(
            src_ref=src_ref, dst_ref=dst_ref, send_sem=send, recv_sem=recv,
            device_id=where, device_id_type=pl.DeviceIdType.MESH,
        )

    right, left, across = dev(xr, y, z, c), dev(xl, y, z, c), dev(x, y, z, sib)
    up, down = dev(x, yr, z, c), dev(x, yl, z, c)

    for n, hbm in enumerate((q_hbm, k_hbm, v_hbm)):
        for j in range(4):
            for h in range(NC):
                pltpu.make_async_copy(
                    hbm.at[pl.ds(h * HALF, HALF), pl.ds(j * HD, HD)], src.at[j, h, n], s_load.at[j, h, n]
                ).start()

    barrier = pltpu.get_barrier_semaphore()
    for k in range(1, NZ * NC):
        other = (z * NC + c + k) % (NZ * NC)
        pl.semaphore_signal(barrier, inc=1, device_id=dev(x, y, other // NC, other % NC), device_id_type=pl.DeviceIdType.MESH)
    for other in (right, left, up, down):
        pl.semaphore_signal(barrier, inc=1, device_id=other, device_id_type=pl.DeviceIdType.MESH)

    acc[...] = jnp.zeros(acc.shape, F32)
    sm[...] = jnp.zeros(sm.shape, F32)
    mx[...] = jnp.full(mx.shape, -1e30, F32)
    for j in range(4):
        for h in range(NC):
            for n in range(3):
                wait_for(src.at[j, h, n], s_load.at[j, h, n])
    pl.semaphore_wait(barrier, NZ * NC - 1 + 4)

    def zof(s):
        return (z + ((s + 1) // 2) * (1 - 2 * ((s + 1) % 2)) + NZ) % NZ

    def send_heads(s, carry):
        zd = zof(s)

        @pl.when(zd // 4 == c)
        def _():
            j = zd - 4 * c
            for k in range(NC):
                cd = (c + 1 - k) % NC

                def go():
                    remote(src.at[j, cd], qkv.at[z, x * NC + cd], s_z.at[j, k], r_z.at[z], dev(x, y, zd, cd)).start()

                if k == 0:
                    go()
                else:
                    pl.when(zd != z)(go)

                    @pl.when(zd == z)
                    def _():
                        pltpu.make_async_copy(src.at[j, cd], qkv.at[z, x * NC + cd], r_z.at[z]).start()

        return carry

    lax.fori_loop(0, NZ, send_heads, 0)

    for n in range(NY):
        pltpu.make_async_copy(
            w_hbm.at[:, pl.ds((n * NC + c) * COLS, COLS)], wb.at[n, c], s_w.at[n]
        ).start()

    def pair(zs, xx, core):
        return qkv.at[zs, xx * NC + core, pl.ds(1, 2)]

    def one(zs, xx, n):
        return qkv.at[zs, xx * NC + c, 1 + n]

    def unit(zq, zk, diagonal):
        query = qkv[zq, x * NC + c, 0]
        key = qkv[zk, :, 1].reshape(KEYS, HD)
        value = qkv[zk, :, 2].reshape(KEYS, HD)
        scores = lax.dot_general(query, key, (((1,), (1,)), ((), ())), preferred_element_type=F32)
        if diagonal:
            row = lax.broadcasted_iota(jnp.int32, scores.shape, 0)
            col = lax.broadcasted_iota(jnp.int32, scores.shape, 1)
            scores = jnp.where(col <= row + (x * NC + c) * HALF, scores, -1e30)
        old = mx[zq]
        new = jnp.maximum(old, jnp.max(scores, axis=1, keepdims=True))
        factor = jnp.exp2((old - new) * C2)
        weights = jnp.exp2((scores - jnp.concatenate([new] * (KEYS // HD), axis=1)) * C2)
        mx[zq] = new
        sm[zq] = sm[zq] * factor + jnp.sum(weights, axis=1, keepdims=True)
        acc[zq] = acc[zq] * factor + jnp.dot(weights.astype(BF16), value, preferred_element_type=F32)

    last = (z + NZ // 2) % NZ

    def send_rows(early):
        def send_out(s, carry):
            zs = zof(NZ - 1 - s)

            @pl.when(zs < last if early else zs >= last)
            def _():
                obuf[zs] = (acc[zs] / sm[zs]).astype(BF16)
                spot = heads.at[pl.ds(c * HALF, HALF), pl.ds(z * HD, HD)]

                @pl.when(zs != z)
                def _():
                    remote(obuf.at[zs], spot, s_o.at[zs], r_o.at[z], dev(x, y, zs, c)).start()

                @pl.when(zs == z)
                def _():
                    pltpu.make_async_copy(obuf.at[zs], spot, r_o.at[z]).start()

            return carry

        lax.fori_loop(0, NZ, send_out, 0)

    def step(s, carry):
        @pl.when(s < NZ)
        def _():
            zs = zof(s)
            mine = pair(zs, x, c)
            wait_for(qkv.at[zs, x * NC + c], r_z.at[zs])
            remote(mine, mine, s_x.at[zs, 0], r_x.at[zs, 0], right).start()
            remote(mine, mine, s_x.at[zs, 1], r_x.at[zs, 1], left).start()
            remote(mine, mine, s_rel.at[zs, 0], r_rel.at[zs, 0], across).start()

        @pl.when((s >= 1) & (s < NZ + 1))
        def _():
            zs = zof(s - 1)
            a = pair(zs, xl, c)
            wait_for(a, r_x.at[zs, 0])
            remote(one(zs, xl, 0), one(zs, xl, 0), s_x.at[zs, 2], r_x.at[zs, 2], right).start()
            remote(a, a, s_rel.at[zs, 1], r_rel.at[zs, 1], across).start()
            b = pair(zs, xr, c)
            wait_for(b, r_x.at[zs, 1])
            remote(one(zs, xr, 1), one(zs, xr, 1), s_x.at[zs, 3], r_x.at[zs, 3], left).start()
            remote(b, b, s_rel.at[zs, 2], r_rel.at[zs, 2], across).start()

        @pl.when((s >= 2) & (s < NZ + 2))
        def _():
            zs = zof(s - 2)
            o = pair(zs, xo, c)
            wait_for(one(zs, xo, 0), r_x.at[zs, 2])
            wait_for(one(zs, xo, 1), r_x.at[zs, 3])
            remote(o, o, s_rel.at[zs, 3], r_rel.at[zs, 3], across).start()

        @pl.when(s >= NZ + 3 - NY)
        def _():
            n = s - (NZ + 3 - NY)
            remote(
                w_hbm.at[:, pl.ds((n * NC + sib) * COLS, COLS)], wb.at[n, c], ss_w.at[n], r_w.at[n], across
            ).start()

        @pl.when(s == NZ + 2)
        def _():
            send_rows(True)

        @pl.when(s >= 3)
        def _():
            t = s - 3
            zs = zof(t)
            for n, xx in enumerate((x, xl, xr, xo)):
                wait_for(pair(zs, xx, sib), r_rel.at[zs, n])
            unit(zs, zs, True)

            def earlier(u, inner):
                zu = zof(u)
                unit(jnp.maximum(zs, zu), jnp.minimum(zs, zu), False)
                return inner

            lax.fori_loop(0, t, earlier, 0)

        return carry

    lax.fori_loop(0, NZ + 3, step, 0)

    send_rows(False)

    def relay_out(s, carry):
        h = zof(s)
        spot = heads.at[pl.ds(c * HALF, HALF), pl.ds(h * HD, HD)]
        wait_for(spot, r_o.at[h])
        remote(spot, spot, s_oc.at[h], r_oc.at[h], across).start()
        return carry

    lax.fori_loop(0, NZ, relay_out, 0)
    for n in range(NY):
        wait_for(wb.at[n, c], s_w.at[n])
        wait_for(wb.at[n, sib], r_w.at[n])

    def await_out(s, carry):
        h = zof(s)
        wait_for(heads.at[pl.ds(sib * HALF, HALF), pl.ds(h * HD, HD)], r_oc.at[h])
        return carry

    lax.fori_loop(0, NZ, await_out, 0)

    def project(n, k):
        cols = slice(k * CHUNK, (k + 1) * CHUNK)
        weight = jnp.concatenate([wb[n, 0, :, cols], wb[n, 1, :, cols]], axis=0)
        return jnp.dot(heads[...], weight, preferred_element_type=F32)

    for k in range(NCH):
        pbuf[0, k] = project(yo, k).astype(BF16)
        remote(pbuf.at[0, k], ropp.at[k], s_p.at[0, k], r_p.at[0, k], up if k < NCH // 2 else down).start()
    half = NCH // 2
    for k in range(half):
        a, b = half + k, k
        pbuf[1, a] = project(yr, a).astype(BF16)
        remote(pbuf.at[1, a], rfin.at[0, a], s_p.at[1, a], r_p.at[1, a], up).start()
        pbuf[2, b] = project(yl, b).astype(BF16)
        remote(pbuf.at[2, b], rfin.at[1, b], s_p.at[2, b], r_p.at[2, b], down).start()
    for k in range(half):
        a, b = k, half + k
        part = project(yr, a)
        wait_for(ropp.at[a], r_p.at[0, a])
        pbuf[1, a] = (part + ropp[a].astype(F32)).astype(BF16)
        remote(pbuf.at[1, a], rfin.at[0, a], s_p.at[1, a], r_p.at[1, a], up).start()
        part = project(yl, b)
        wait_for(ropp.at[b], r_p.at[0, b])
        pbuf[2, b] = (part + ropp[b].astype(F32)).astype(BF16)
        remote(pbuf.at[2, b], rfin.at[1, b], s_p.at[2, b], r_p.at[2, b], down).start()
    order = [2, 0, 3, 1]
    for k in order:
        part = project(y, k)
        wait_for(rfin.at[0, k], r_p.at[1, k])
        wait_for(rfin.at[1, k], r_p.at[2, k])
        out_ref[:, k * CHUNK : (k + 1) * CHUNK] = (
            part + rfin[0, k].astype(F32) + rfin[1, k].astype(F32)
        ).astype(BF16)

    def drain(s, carry):
        zs = zof(s)

        @pl.when(zs // 4 == c)
        def _():
            j = zs - 4 * c
            wait_for(src.at[j, sib], s_z.at[j, 0])

            @pl.when(zs != z)
            def _():
                wait_for(src.at[j, c], s_z.at[j, 1])

        for n, xx in enumerate((x, x, xl, xr)):
            wait_for(pair(zs, xx, c) if n < 2 else one(zs, xx, n - 2), s_x.at[zs, n])
        for n, xx in enumerate((x, xl, xr, xo)):
            wait_for(pair(zs, xx, c), s_rel.at[zs, n])

        @pl.when(zs != z)
        def _():
            wait_for(obuf.at[zs], s_o.at[zs])

        wait_for(heads.at[pl.ds(c * HALF, HALF), pl.ds(zs * HD, HD)], s_oc.at[zs])
        return carry

    lax.fori_loop(0, NZ, drain, 0)
    for n in range(NY):
        wait_for(w_hbm.at[:, pl.ds((n * NC + sib) * COLS, COLS)], ss_w.at[n])
    for k in range(NCH):
        for n in range(3):
            wait_for(pbuf.at[n, k], s_p.at[n, k])


def per_device(attn_query, attn_key, attn_value, out_weight):
    dma = pltpu.SemaphoreType.DMA
    anywhere = pl.BlockSpec(memory_space=pl.ANY)
    return pl.pallas_call(
        kernel,
        out_shape=jax.ShapeDtypeStruct((ROWS, COLS), BF16),
        in_specs=[anywhere] * 4,
        out_specs=pl.BlockSpec(memory_space=pltpu.VMEM),
        scratch_shapes=[
            pltpu.VMEM((4, NC, 3, HALF, HD), BF16),
            pltpu.VMEM((NZ, NX * NC, 3, HALF, HD), BF16),
            pltpu.VMEM((NY, NC, 512, COLS), BF16),
            pltpu.VMEM((ROWS, NZ * HD), BF16),
            pltpu.VMEM((NZ, HALF, HD), BF16),
            pltpu.VMEM((NZ, HALF, HD), F32),
            pltpu.VMEM((NZ, HALF, HD), F32),
            pltpu.VMEM((NZ, HALF, HD), F32),
            pltpu.VMEM((3, NCH, ROWS, CHUNK), BF16),
            pltpu.VMEM((NCH, ROWS, CHUNK), BF16),
            pltpu.VMEM((2, NCH, ROWS, CHUNK), BF16),
            dma((4, NC, 3)), dma((NY,)), dma((NY,)), dma((NY,)),
            dma((4, NC)), dma((NZ,)),
            dma((NZ, 4)), dma((NZ, 4)), dma((NZ, 4)), dma((NZ, 4)),
            dma((NZ,)), dma((NZ,)), dma((NZ,)), dma((NZ,)),
            dma((3, NCH)), dma((3, NCH)),
        ],
        compiler_params=pltpu.CompilerParams(
            collective_id=0, has_side_effects=True, vmem_limit_bytes=56 << 20
        ),
        name="attention",
    )(attn_query, attn_key, attn_value, out_weight)


def solution(mesh):
    return jax.shard_map(
        per_device,
        mesh=mesh,
        in_specs=(P("ctx", "tp"), P("ctx", "tp"), P("ctx", "tp"), P("tp", None)),
        out_specs=P("ctx", "tp"),
        check_vma=False,
    )
```
